32 devices in a mesh: seq: 8 (over z, x), head: 4 (over y, core).
Axes of the slice: x: 2, y: 2, z: 4, core: 2. Of those that a mesh axis runs over, the one named last changes fastest.
Arguments:
- block_order: int32 [16], replicated, may hold values from 0 to 15, each once
- queries: bfloat16 [2048, 4096], P('seq', 'head'), may hold values from -52 to 52
- keys: bfloat16 [2048, 4096], P('seq', 'head'), may hold values from -4.5 to 4.5
- values: bfloat16 [2048, 4096], P('seq', 'head'), may hold values from -5 to 5
- hyena_q: bfloat16 [2048, 4096], P('seq', 'head'), may hold values from -5 to 5
- hyena_k: bfloat16 [2048, 4096], P('seq', 'head'), may hold values from -5 to 5
- hyena_v: bfloat16 [2048, 4096], P('seq', 'head'), may hold values from -5 to 5
- hyena_grad: bfloat16 [2048, 4096], P('seq', 'head'), may hold values from -5 to 5
- filters: float32 [256, 128], P('head'), may hold values from -0.5 to 0.5
- proj_weight: bfloat16 [3, 4096, 4096], P(None, None, 'head'), may hold values from -0.0546875 to 0.0546875
Outputs:
- input_grad: bfloat16 [2048, 4096], P('seq', 'head')
- query_grad: bfloat16 [2048, 4096], P('seq', 'head')
- key_grad: bfloat16 [2048, 4096], P('seq', 'head')
- value_grad: bfloat16 [2048, 4096], P('seq', 'head')
The draws below stay inside these ranges and needn't reach their ends.
Inputs may be any that keep to these rules, and one draw needn't show every extreme that they name: `block_order`: A permutation of the sequence blocks; entry 2 d + j is the position block of rows d * 256 + j * 128 to d * 256 + j * 128 + 127.
All inputs are finite; a program needn't handle non-finite values.
Results may differ from the reference program's by a relative error of at most 0.01.
Values may be sent and summed in bfloat16 or wider, within the bound.
A program may use at most 128 MiB of HBM per device.

```python
import jax
import jax.numpy as jnp
from jax import lax

D = 4096
HD = 128
HEADS = 32
GROUP = 16
GROUPS = 256
KL = 128
BLOCK = 128
BLOCKS = 16
TOKENS = 2048


def attention_pair(key):
    base_key = jax.random.fold_in(key, 101)
    query_key, key_key = jax.random.split(base_key, 2)
    shape = (TOKENS, HEADS, HD)
    key_rows = jnp.clip(jax.random.normal(key_key, shape, jnp.float32), -4.5, 4.5)
    query_rows = jnp.clip(jax.random.normal(query_key, shape, jnp.float32), -4.5, 4.5)
    return (query_rows.reshape(TOKENS, D), key_rows.reshape(TOKENS, D))


def draw_queries(key, part):
    return attention_pair(key)[0].astype(jnp.bfloat16)


def draw_keys(key, part):
    return attention_pair(key)[1].astype(jnp.bfloat16)


def levels(key, dims, shards, low, high):
    def one(axis_at, shards_of):
        steps = jax.random.uniform(jax.random.fold_in(jax.random.fold_in(key, 6), axis_at), (shards_of,), jnp.float32, low / len(shards), high / len(shards))
        return jnp.repeat(jnp.exp(steps), dims[axis_at] // shards_of).reshape((-1,) + (1,) * (len(dims) - axis_at - 1))

    gain = one(*shards[0])
    for cut in shards[1:]:
        gain = gain * one(*cut)
    return gain


def gaussian(rng, dims, spread, most, pieces=(), kind=jnp.bfloat16):
    entries = spread * jax.random.normal(rng, dims, jnp.float32)
    if pieces:
        entries = entries * levels(rng, dims, pieces, -0.22, 0.18)
    return jnp.clip(entries, -most, most).astype(kind)


def setup_inputs(seed: int = 0) -> dict:
    key_of = jax.random.split(jax.random.key(seed), 11)
    block_order = jax.random.permutation(key_of[0], BLOCKS).astype(jnp.int32)
    queries = draw_queries(jax.random.fold_in(key_of[10], 71), 0)
    keys = draw_keys(jax.random.fold_in(key_of[10], 71), 0)
    values = gaussian(key_of[3], (TOKENS, D), 1.0, 5.0, ((0, 8), (1, 4)))
    hyena_q = gaussian(key_of[4], (TOKENS, D), 1.0, 5.0, ((0, 8), (1, 4)))
    hyena_k = gaussian(key_of[5], (TOKENS, D), 1.0, 5.0, ((0, 8), (1, 4)))
    hyena_v = gaussian(key_of[6], (TOKENS, D), 1.0, 5.0, ((0, 8), (1, 4)))
    hyena_grad = gaussian(key_of[7], (TOKENS, D), 1.0, 5.0, ((0, 8), (1, 4)))
    filters = gaussian(key_of[8], (GROUPS, KL), KL ** -0.5, 0.5, ((0, 4),), jnp.float32)
    proj_weight = gaussian(key_of[9], (3, D, D), (3 * D) ** -0.5, 0.0546875, ((2, 4),))
    return dict(block_order=block_order, queries=queries, keys=keys, values=values, hyena_q=hyena_q, hyena_k=hyena_k, hyena_v=hyena_v, hyena_grad=hyena_grad, filters=filters, proj_weight=proj_weight)


def reference(block_order, queries, keys, values, hyena_q, hyena_k, hyena_v, hyena_grad, filters, proj_weight):
    row_ids = jnp.arange(TOKENS, dtype=jnp.int32)
    position = (block_order[row_ids // BLOCK] * BLOCK + row_ids % BLOCK).astype(jnp.int32)
    in_order = jnp.argsort(position).astype(jnp.int32)
    product_kv = (hyena_k.astype(jnp.float32) * hyena_v.astype(jnp.float32)).astype(jnp.bfloat16)
    product_dq = (hyena_grad.astype(jnp.float32) * hyena_q.astype(jnp.float32)).astype(jnp.bfloat16)
    series_z = product_kv[in_order].astype(jnp.float32)
    series_dc = product_dq[in_order].astype(jnp.float32)
    tap_table = jnp.repeat(filters, GROUP, axis=0).T
    padded_z = jnp.pad(series_z, ((KL, 0), (0, 0)))
    padded_dc = jnp.pad(series_dc, ((0, KL), (0, 0)))

    def add_tap(partial_sums, tap_index):
        conv_sum, back_sum = partial_sums
        tap_weights = lax.dynamic_index_in_dim(tap_table, tap_index, 0, keepdims=False)
        conv_sum = conv_sum + tap_weights * lax.dynamic_slice_in_dim(padded_z, KL - tap_index, TOKENS, 0)
        back_sum = back_sum + tap_weights * lax.dynamic_slice_in_dim(padded_dc, tap_index, TOKENS, 0)
        return (conv_sum, back_sum), None

    zeros_field = jnp.zeros((TOKENS, D), jnp.float32)
    scanned = lax.scan(add_tap, (zeros_field, zeros_field), jnp.arange(KL, dtype=jnp.int32))
    conv_pos, back_pos = scanned[0]
    convolved = conv_pos[position]
    back_conv = back_pos[position]
    stacked = jnp.stack([hyena_grad.astype(jnp.float32) * convolved,
                         back_conv * hyena_v.astype(jnp.float32),
                         back_conv * hyena_k.astype(jnp.float32)]).astype(jnp.bfloat16)
    summed = jnp.zeros((TOKENS, D), jnp.float32)
    for member in range(3):
        summed = summed + jnp.dot(stacked[member], proj_weight[member].T, preferred_element_type=jnp.float32)
    input_grad = summed.astype(jnp.bfloat16)

    visible = position[None, :] <= position[:, None]
    score_scale = HD ** -0.5

    def split_heads(array):
        return array.reshape(TOKENS, HEADS, HD).transpose(1, 0, 2)

    def head_grads(operands):
        query_h, key_h, value_h, output_grad = operands
        scores = jnp.dot(query_h, key_h.T, preferred_element_type=jnp.float32) * score_scale
        scores = jnp.where(visible, scores, -1e30)
        row_top = jnp.max(scores, axis=1, keepdims=True)
        exponent_terms = jnp.where(visible, jnp.exp(scores - row_top), 0.0)
        probabilities = exponent_terms / jnp.sum(exponent_terms, axis=1, keepdims=True)
        prob_grad = jnp.dot(output_grad, value_h.T, preferred_element_type=jnp.float32)
        row_delta = jnp.sum(probabilities * prob_grad, axis=1, keepdims=True)
        score_grad = probabilities * (prob_grad - row_delta)
        probs_low = probabilities.astype(jnp.bfloat16)
        score_low = score_grad.astype(jnp.bfloat16)
        grad_query = (jnp.dot(score_low, key_h, preferred_element_type=jnp.float32) * score_scale).astype(jnp.bfloat16)
        grad_key = (jnp.dot(score_low.T, query_h, preferred_element_type=jnp.float32) * score_scale).astype(jnp.bfloat16)
        grad_value = jnp.dot(probs_low.T, output_grad, preferred_element_type=jnp.float32).astype(jnp.bfloat16)
        return grad_query, grad_key, grad_value

    head_results = lax.map(head_grads, (split_heads(queries), split_heads(keys), split_heads(values), split_heads(input_grad)))

    def join_heads(array):
        return array.transpose(1, 0, 2).reshape(TOKENS, D)

    return input_grad, join_heads(head_results[0]), join_heads(head_results[1]), join_heads(head_results[2])
```

```python
import functools

import jax
import jax.numpy as jnp
from jax import lax
from jax.experimental import pallas as pl
from jax.experimental.pallas import tpu as pltpu
from jax.sharding import PartitionSpec as P

HD = 128
GROUP = 16
KL = 128
BLOCK = 128


def for_sending(x):

    def short(part):
        return part.astype(jnp.bfloat16) if part.dtype == jnp.float32 else part

    return jax.tree.map(short, x)


def passed_along(value, axis, steps):
    count = lax.axis_size(axis)
    pairs = [(source, (source + steps) % count) for source in range(count)]
    return lax.ppermute(value, axis, pairs)


def keep_state(current):
    return current


def ring_device(
    block_order, queries, keys, values, hyena_q, hyena_k, hyena_v, hyena_grad, filters, proj_weight
):
    seq_count = lax.axis_size("seq")
    my_index = lax.axis_index("seq")
    row_count = queries.shape[0]
    feature_width = queries.shape[1]
    head_count = feature_width // HD
    block_total = block_order.shape[0]
    offsets = jnp.arange(BLOCK, dtype=jnp.int32)
    block_ids = jnp.arange(block_total, dtype=jnp.int32)

    def block_positions(source):
        block_pair = lax.dynamic_slice_in_dim(block_order, 2 * source, 2)
        return jnp.concatenate([block_pair[0] * BLOCK + offsets, block_pair[1] * BLOCK + offsets])

    def holder_of(target):
        return jnp.sum(jnp.where(block_order == target, block_ids, 0))

    my_positions = block_positions(my_index)
    product_kv = (hyena_k.astype(jnp.float32) * hyena_v.astype(jnp.float32)).astype(jnp.bfloat16)
    product_dq = (hyena_grad.astype(jnp.float32) * hyena_q.astype(jnp.float32)).astype(jnp.bfloat16)
    my_blocks = [
        lax.dynamic_index_in_dim(block_order, 2 * my_index + portion, 0, keepdims=False)
        for portion in range(2)
    ]
    gathered_z, gathered_dc = (
        lax.all_gather(product_kv, "seq", axis=0, tiled=True),
        lax.all_gather(product_dq, "seq", axis=0, tiled=True),
    )
    group_count = filters.shape[0]
    channels = hyena_q.shape[1]
    out_rows = jnp.arange(BLOCK)[:, None, None]
    window_rows = jnp.arange(BLOCK + KL)[None, :, None]
    tap_ids = jnp.arange(KL)[None, None, :]
    causal_table = (out_rows + KL - window_rows == tap_ids).astype(jnp.float32)
    anti_table = (window_rows - out_rows == tap_ids).astype(jnp.float32)
    causal_toeplitz = jnp.einsum(
        "gj,tsj->gts", filters, causal_table, precision=lax.Precision.HIGHEST
    )
    anti_toeplitz = jnp.einsum("gj,tsj->gts", filters, anti_table, precision=lax.Precision.HIGHEST)

    def apply_groups(toeplitz, window):
        grouped = window.astype(jnp.float32).reshape(BLOCK + KL, group_count, GROUP)
        result = jnp.einsum("gts,sgk->tgk", toeplitz, grouped, precision=lax.Precision.HIGHEST)
        return result.reshape(BLOCK, channels)

    conv_parts = []
    back_parts = []
    for portion in range(2):
        block_id = my_blocks[portion]
        before = lax.dynamic_slice_in_dim(
            gathered_z, holder_of(block_id - 1) * BLOCK + BLOCK - KL, KL, 0
        )
        before = jnp.where(block_id >= 1, before, jnp.zeros_like(before))
        after = lax.dynamic_slice_in_dim(gathered_dc, holder_of(block_id + 1) * BLOCK, KL, 0)
        after = jnp.where(block_id + 1 < block_total, after, jnp.zeros_like(after))
        own_z = product_kv[portion * BLOCK : (portion + 1) * BLOCK]
        own_dc = product_dq[portion * BLOCK : (portion + 1) * BLOCK]
        conv_parts.append(apply_groups(causal_toeplitz, jnp.concatenate([before, own_z])))
        back_parts.append(apply_groups(anti_toeplitz, jnp.concatenate([own_dc, after])))
    convolved = jnp.concatenate(conv_parts)
    back_conv = jnp.concatenate(back_parts)
    stacked = jnp.stack(
        [
            hyena_grad.astype(jnp.float32) * convolved,
            back_conv * hyena_v.astype(jnp.float32),
            back_conv * hyena_k.astype(jnp.float32),
        ]
    ).astype(jnp.bfloat16)
    summed = lax.psum_scatter(
        jnp.einsum("mic,mtc->it", proj_weight, stacked, preferred_element_type=jnp.float32),
        "head",
        scatter_dimension=0,
        tiled=True,
    )
    input_grad = summed.T.astype(jnp.bfloat16)
    score_scale = HD ** (-0.5)
    query_heads = queries.reshape(row_count, head_count, HD)
    key_heads = keys.reshape(row_count, head_count, HD)
    value_heads = values.reshape(row_count, head_count, HD)
    grad_heads = input_grad.reshape(row_count, head_count, HD)

    def tile_scores(query_block, key_block, query_pos, key_pos):
        scores = (
            jnp.einsum("qhd,khd->hqk", query_block, key_block, preferred_element_type=jnp.float32)
            * score_scale
        )
        allowed = (key_pos[None, :] <= query_pos[:, None])[None]
        return (scores, allowed)

    def stat_update(running, key_block, value_block, source):
        key_pos = block_positions(source)
        active = jnp.min(key_pos) <= jnp.max(my_positions)

        def stat_accumulate(current):
            row_max, row_sum, row_dot = current
            scores, allowed = tile_scores(query_heads, key_block, my_positions, key_pos)
            masked = jnp.where(allowed, scores, -1e30)
            new_max = jnp.maximum(row_max, jnp.max(masked, axis=2))
            terms = jnp.where(allowed, jnp.exp(masked - new_max[:, :, None]), 0.0)
            prob_grad = jnp.einsum(
                "qhd,khd->hqk", grad_heads, value_block, preferred_element_type=jnp.float32
            )
            factor = jnp.exp(row_max - new_max)
            return (
                new_max,
                row_sum * factor + jnp.sum(terms, axis=2),
                row_dot * factor + jnp.sum(terms * prob_grad, axis=2),
            )

        return lax.cond(active, stat_accumulate, keep_state, running)

    initial = (
        jnp.full((head_count, row_count), -1e30, jnp.float32),
        jnp.zeros((head_count, row_count), jnp.float32),
        jnp.zeros((head_count, row_count), jnp.float32),
    )

    def tile_grads(
        query_block, grad_block, norm_block, delta_block, query_pos, key_block, value_block, key_pos
    ):
        scores, allowed = tile_scores(query_block, key_block, query_pos, key_pos)
        probabilities = jnp.where(allowed, jnp.exp(scores - norm_block[:, :, None]), 0.0)
        prob_grad = jnp.einsum(
            "qhd,khd->hqk", grad_block, value_block, preferred_element_type=jnp.float32
        )
        score_grad = probabilities * (prob_grad - delta_block[:, :, None])
        probs_low = probabilities.astype(jnp.bfloat16)
        score_low = score_grad.astype(jnp.bfloat16)
        add_query = (
            jnp.einsum("hqk,khd->qhd", score_low, key_block, preferred_element_type=jnp.float32)
            * score_scale
        )
        add_key = (
            jnp.einsum("hqk,qhd->khd", score_low, query_block, preferred_element_type=jnp.float32)
            * score_scale
        )
        add_value = jnp.einsum(
            "hqk,qhd->khd", probs_low, grad_block, preferred_element_type=jnp.float32
        )
        return (add_query, add_key, add_value)

    zero_rows = jnp.zeros((row_count, head_count, HD), jnp.float32)

    def move_stat_queries(pair):
        return jax.tree.map(
            lambda part, own: part.astype(own.dtype),
            passed_along(for_sending(pair), "seq", 1),
            pair,
        )

    def stat_turn(turn_index, loop_state):
        running, key_block, value_block = loop_state
        source = (my_index - turn_index) % seq_count
        running = stat_update(running, key_block, value_block, source)
        key_block, value_block = move_stat_queries((key_block, value_block))
        return (running, key_block, value_block)

    loop_state = lax.fori_loop(0, seq_count - 1, stat_turn, (initial, key_heads, value_heads))
    running = stat_update(
        loop_state[0], loop_state[1], loop_state[2], (my_index - (seq_count - 1)) % seq_count
    )
    log_norm = running[0] + jnp.log(running[1])
    row_delta = running[2] / running[1]

    def query_turn(turn_index, loop_state):
        query_block, grad_block, norm_block, delta_block, query_acc, key_acc, value_acc = loop_state
        source = (my_index - turn_index) % seq_count
        query_pos = block_positions(source)
        active = jnp.min(my_positions) <= jnp.max(query_pos)

        def query_accumulate(current):
            add_query, add_key, add_value = tile_grads(
                query_block,
                grad_block,
                norm_block,
                delta_block,
                query_pos,
                key_heads,
                value_heads,
                my_positions,
            )
            return (current[0] + add_query, current[1] + add_key, current[2] + add_value)

        query_acc, key_acc, value_acc = lax.cond(
            active, query_accumulate, keep_state, (query_acc, key_acc, value_acc)
        )
        query_block, grad_block = passed_along((query_block, grad_block), "seq", 1)
        norm_block, delta_block, query_acc = passed_along(
            (norm_block, delta_block, query_acc), "seq", 1
        )
        return (query_block, grad_block, norm_block, delta_block, query_acc, key_acc, value_acc)

    final_state = lax.fori_loop(
        0,
        seq_count,
        query_turn,
        (query_heads, grad_heads, log_norm, row_delta, zero_rows, zero_rows, zero_rows),
    )
    query_total = final_state[4]
    key_total = final_state[5]
    value_total = final_state[6]
    query_grad = query_total.reshape(row_count, feature_width).astype(jnp.bfloat16)
    key_grad = key_total.reshape(row_count, feature_width).astype(jnp.bfloat16)
    value_grad = value_total.reshape(row_count, feature_width).astype(jnp.bfloat16)
    return (input_grad, query_grad, key_grad, value_grad)


MESH = pl.DeviceIdType.MESH
VMEM_SPEC = pl.BlockSpec(memory_space=pltpu.VMEM)
SMEM_SPEC = pl.BlockSpec(memory_space=pltpu.SMEM)


def aligned(index, size):
    return pl.ds(pl.multiple_of(index * size, size), size)


def greet(me, n):
    barrier = pltpu.get_barrier_semaphore()
    for step in range(1, n):
        pl.semaphore_signal(
            barrier, inc=1, device_id={"seq": lax.rem(me + step, n)}, device_id_type=MESH
        )
    pl.semaphore_wait(barrier, n - 1)


def exchange(n, me, rows, send_sem, recv_sem, own_sem):
    def parts(to_columns, src, dst, peer):
        if to_columns:
            return src.at[:, aligned(peer, HD)], dst.at[aligned(me, rows), :]
        return src.at[aligned(peer, rows), :], dst.at[:, aligned(me, HD)]

    def remote(tensor, to_columns, src, dst, step):
        peer = lax.rem(me + step, n)
        part, place = parts(to_columns, src, dst, peer)
        return pltpu.make_async_remote_copy(
            src_ref=part,
            dst_ref=place,
            send_sem=send_sem.at[tensor, step],
            recv_sem=recv_sem.at[tensor, step],
            device_id={"seq": peer},
            device_id_type=MESH,
        )

    def own(tensor, to_columns, src, dst):
        part, place = parts(to_columns, src, dst, me)
        return pltpu.make_async_copy(part, place, own_sem.at[tensor])

    def start(tensor, to_columns, src, dst):
        for step in range(1, n):
            remote(tensor, to_columns, src, dst, step).start()
        own(tensor, to_columns, src, dst).start()

    def wait(tensor, to_columns, src, dst):
        for step in range(1, n):
            remote(tensor, to_columns, src, dst, step).wait()
        own(tensor, to_columns, src, dst).wait()

    return remote, own, start, wait


def exchange_sems(tensors, n):
    return [
        pltpu.SemaphoreType.DMA((tensors, n)),
        pltpu.SemaphoreType.DMA((tensors, n)),
        pltpu.SemaphoreType.DMA((tensors,)),
    ]


def move_kernel(n, to_columns, count, *refs):
    sources, targets = refs[:count], refs[count : 2 * count]
    me = lax.axis_index("seq")
    rows = sources[0].shape[0] if to_columns else targets[0].shape[0]
    _, _, start, wait = exchange(n, me, rows, *refs[2 * count :])
    greet(me, n)
    for t in range(count):
        start(t, to_columns, sources[t], targets[t])
    for t in range(count):
        wait(t, to_columns, sources[t], targets[t])


def move(n, to_columns, arrays, collective_id):
    rows, columns = arrays[0].shape
    shape = (rows * n, columns // n) if to_columns else (rows // n, columns * n)
    count = len(arrays)
    return pl.pallas_call(
        functools.partial(move_kernel, n, to_columns, count),
        out_shape=[jax.ShapeDtypeStruct(shape, a.dtype) for a in arrays],
        in_specs=[VMEM_SPEC] * count,
        out_specs=[VMEM_SPEC] * count,
        scratch_shapes=exchange_sems(count, n),
        compiler_params=pltpu.CompilerParams(
            collective_id=collective_id, has_side_effects=True
        ),
    )(*arrays)


def hyena_kernel(
    n, groups, before_ref, after_ref, z_ref, dc_ref, causal_ref, anti_ref, q_ref, k_ref, v_ref,
    conv_ref, dz_ref, qc_ref, kc_ref, vc_ref,
    zc, dcc, convc, dzc, causal_high, causal_low, anti_high, anti_low, send_sem, recv_sem, own_sem,
):
    me = lax.axis_index("seq")
    rows = z_ref.shape[0]
    blocks = zc.shape[0] // BLOCK
    remote, own, start, wait = exchange(n, me, rows, send_sem, recv_sem, own_sem)
    greet(me, n)
    start(0, True, z_ref, zc)
    start(1, True, dc_ref, dcc)

    window = 2 * BLOCK
    for base_ref, high, low in (
        (causal_ref, causal_high, causal_low), (anti_ref, anti_high, anti_low)
    ):
        for g in range(groups):
            base = jnp.broadcast_to(base_ref[g : g + 1, :], (BLOCK, window))
            table = pltpu.roll(base, 0, 1, stride=1, stride_axis=0)
            top = table.astype(jnp.bfloat16)
            high[:, g * window : (g + 1) * window] = top
            low[:, g * window : (g + 1) * window] = (table - top.astype(jnp.float32)).astype(
                jnp.bfloat16
            )

    lane_group = lax.broadcasted_iota(jnp.int32, (window, 2 * HD), 1) % HD // GROUP

    def filtered(source, neighbours, high, low, target, place, own_first):
        halves = []
        for half in range(2):
            block = place * 2 + half
            own_rows = source[aligned(block, BLOCK), :]
            picks = neighbours[aligned(block, blocks), :]
            other = source[:BLOCK, :] * picks[0:1, :]
            for b in range(1, blocks):
                other = other + source[b * BLOCK : (b + 1) * BLOCK, :] * picks[b : b + 1, :]
            pair = [own_rows, other] if own_first else [other, own_rows]
            halves.append(jnp.concatenate(pair, axis=0))
        wide = jnp.concatenate(halves, axis=1)
        stack = jnp.concatenate(
            [jnp.where(lane_group == g, wide, jnp.zeros_like(wide)) for g in range(groups)], axis=0
        )
        result = jnp.dot(high[...], stack, preferred_element_type=jnp.float32)
        result = result + jnp.dot(low[...], stack, preferred_element_type=jnp.float32)
        result = result.astype(target.dtype)
        target[aligned(place, rows), :] = jnp.concatenate(
            [result[:, :HD], result[:, HD:]], axis=0
        )

    def send_back(tensor, source, neighbours, high, low, target, out, own_first):
        def one(step, carry):
            filtered(source, neighbours, high, low, target, lax.rem(me + step, n), own_first)
            remote(tensor, False, target, out, step).start()
            return carry

        lax.fori_loop(1, n, one, 0)
        filtered(source, neighbours, high, low, target, me, own_first)
        own(tensor, False, target, out).start()

    wait(0, True, z_ref, zc)
    send_back(2, zc, before_ref, causal_high, causal_low, convc, conv_ref, False)
    wait(1, True, dc_ref, dcc)
    send_back(3, dcc, after_ref, anti_high, anti_low, dzc, dz_ref, True)
    attention = ((4, q_ref, qc_ref), (5, k_ref, kc_ref), (6, v_ref, vc_ref))
    for t, src, dst in attention:
        start(t, True, src, dst)
    wait(2, False, convc, conv_ref)
    wait(3, False, dzc, dz_ref)
    for t, src, dst in attention:
        wait(t, True, src, dst)


def hyena(n, before, after, z, dc, causal_base, anti_base, queries, keys, values):
    rows, columns = z.shape
    groups = causal_base.shape[0]
    like = jax.ShapeDtypeStruct(z.shape, jnp.bfloat16)
    moved = jax.ShapeDtypeStruct((rows * n, HD), jnp.bfloat16)
    table = pltpu.VMEM((BLOCK, groups * 2 * BLOCK), jnp.bfloat16)
    return pl.pallas_call(
        functools.partial(hyena_kernel, n, groups),
        out_shape=[like, like, moved, moved, moved],
        in_specs=[VMEM_SPEC] * 9,
        out_specs=[VMEM_SPEC] * 5,
        scratch_shapes=[pltpu.VMEM((rows * n, HD), jnp.bfloat16)] * 4
        + [table] * 4
        + exchange_sems(7, n),
        compiler_params=pltpu.CompilerParams(collective_id=0, has_side_effects=True),
    )(before, after, z, dc, causal_base, anti_base, queries, keys, values)


def attention_kernel(
    order_ref, holder_ref, q_ref, k_ref, v_ref, g_ref, dq_ref, dk_ref, dv_ref,
    ks, vs, kst, dq_sum, dk_sum, dv_sum,
):
    blocks = order_ref.shape[0]
    scale = HD ** (-0.5)
    tile = 2 * BLOCK
    for b in range(blocks):
        at = aligned(holder_ref[b], BLOCK)
        here = slice(b * BLOCK, (b + 1) * BLOCK)
        rows = k_ref[at, :]
        ks[here, :] = rows
        kst[:, here] = rows.T
        vs[here, :] = v_ref[at, :]
    contract_last = (((1,), (1,)), ((), ()))
    for i in reversed(range(blocks // 2)):
        width = (i + 1) * tile
        first = aligned(holder_ref[2 * i], BLOCK)
        second = aligned(holder_ref[2 * i + 1], BLOCK)
        q = jnp.concatenate([q_ref[first, :], q_ref[second, :]], axis=0)
        g = jnp.concatenate([g_ref[first, :], g_ref[second, :]], axis=0)
        scores = lax.dot_general(
            ks[:width, :], q, contract_last, preferred_element_type=jnp.float32
        ) * scale
        key_at = lax.broadcasted_iota(jnp.int32, (tile, tile), 0)
        query_at = lax.broadcasted_iota(jnp.int32, (tile, tile), 1)
        last = jnp.where(key_at <= query_at, scores[width - tile :], -1e30)
        if i:
            scores = jnp.concatenate([scores[: width - tile], last], axis=0)
        else:
            scores = last
        top = jnp.max(scores, axis=0, keepdims=True)
        terms = jnp.exp(scores - top)
        inverse = 1.0 / jnp.sum(terms, axis=0, keepdims=True)
        prob = terms * inverse
        prob_grad = lax.dot_general(
            vs[:width, :], g, contract_last, preferred_element_type=jnp.float32
        )
        delta = jnp.sum(prob * prob_grad, axis=0, keepdims=True)
        score_grad = (prob * (prob_grad - delta)).astype(jnp.bfloat16)
        add_value = jnp.dot(prob.astype(jnp.bfloat16), g, preferred_element_type=jnp.float32)
        add_key = jnp.dot(score_grad, q, preferred_element_type=jnp.float32)
        if i == blocks // 2 - 1:
            dv_sum[:width, :] = add_value
            dk_sum[:width, :] = add_key
        else:
            dv_sum[:width, :] += add_value
            dk_sum[:width, :] += add_key
        query_t = jnp.dot(kst[:, :width], score_grad, preferred_element_type=jnp.float32)
        dq_sum[i * tile : (i + 1) * tile, :] = query_t.T * scale
    for s in range(blocks):
        at = aligned(order_ref[s], BLOCK)
        here = slice(s * BLOCK, (s + 1) * BLOCK)
        dq_ref[here, :] = dq_sum[at, :].astype(dq_ref.dtype)
        dk_ref[here, :] = (dk_sum[at, :] * scale).astype(dk_ref.dtype)
        dv_ref[here, :] = dv_sum[at, :].astype(dv_ref.dtype)


def attention(order, holder, q, k, v, g):
    shape = jax.ShapeDtypeStruct(q.shape, jnp.bfloat16)
    low = pltpu.VMEM(q.shape, jnp.bfloat16)
    full = pltpu.VMEM(q.shape, jnp.float32)
    return pl.pallas_call(
        attention_kernel,
        out_shape=[shape] * 3,
        in_specs=[SMEM_SPEC] * 2 + [VMEM_SPEC] * 4,
        out_specs=[VMEM_SPEC] * 3,
        scratch_shapes=[low, low, pltpu.VMEM(q.shape[::-1], jnp.bfloat16), full, full, full],
    )(order, holder, q, k, v, g)


def column_device(
    block_order, queries, keys, values, hyena_q, hyena_k, hyena_v, hyena_grad, filters, proj_weight
):
    n = lax.axis_size("seq")
    me = lax.axis_index("seq")
    blocks = block_order.shape[0]
    ids = jnp.arange(blocks, dtype=jnp.int32)
    holder = jnp.sum(
        jnp.where(block_order[None, :] == ids[:, None], ids[None, :], 0), axis=1
    ).astype(jnp.int32)

    def neighbour(offset):
        found = (block_order[None, :] == block_order[:, None] + offset).astype(jnp.bfloat16)
        return jnp.broadcast_to(found.reshape(blocks * blocks, 1), (blocks * blocks, HD))

    z = (hyena_k.astype(jnp.float32) * hyena_v.astype(jnp.float32)).astype(jnp.bfloat16)
    dc = (hyena_grad.astype(jnp.float32) * hyena_q.astype(jnp.float32)).astype(jnp.bfloat16)
    groups = filters.shape[0] // n
    taps = lax.dynamic_slice_in_dim(filters, me * groups, groups, 0)
    anti_base = jnp.pad(taps, ((0, 0), (0, KL)))
    causal_base = jnp.pad(taps[:, ::-1], ((0, 0), (1, KL - 1)))
    convolved, back_conv, qc, kc, vc = hyena(
        n, neighbour(-1), neighbour(1), z, dc, causal_base, anti_base, queries, keys, values
    )
    convolved = convolved.astype(jnp.float32)
    back_conv = back_conv.astype(jnp.float32)
    stacked = jnp.stack(
        [
            hyena_grad.astype(jnp.float32) * convolved,
            back_conv * hyena_v.astype(jnp.float32),
            back_conv * hyena_k.astype(jnp.float32),
        ]
    ).astype(jnp.bfloat16)
    summed = lax.psum_scatter(
        jnp.einsum("mtc,mic->ti", stacked, proj_weight, preferred_element_type=jnp.float32),
        "head",
        scatter_dimension=1,
        tiled=True,
    )
    input_grad = summed.astype(jnp.bfloat16)
    (gc,) = move(n, True, [input_grad], 1)
    grads = attention(block_order, holder, qc, kc, vc, gc)
    query_grad, key_grad, value_grad = move(n, False, list(grads), 2)
    return (input_grad, query_grad, key_grad, value_grad)


def per_device(*arrays):
    queries, filters = arrays[1], arrays[8]
    n = lax.axis_size("seq")
    whole_heads = queries.shape[1] == n * HD and queries.shape[0] == 2 * BLOCK
    if whole_heads and filters.shape[0] % n == 0 and KL == BLOCK == HD:
        return column_device(*arrays)
    return ring_device(*arrays)


def solution(mesh):
    placed = (
        P(),
        P("seq", "head"),
        P("seq", "head"),
        P("seq", "head"),
        P("seq", "head"),
        P("seq", "head"),
        P("seq", "head"),
        P("seq", "head"),
        P("head", None),
        P(None, None, "head"),
    )
    return jax.shard_map(
        per_device,
        mesh=mesh,
        in_specs=placed,
        out_specs=(P("seq", "head"), P("seq", "head"), P("seq", "head"), P("seq", "head")),
        check_vma=False,
    )
```

```python
import functools

import jax
import jax.numpy as jnp
from jax import lax
from jax.experimental import pallas as pl
from jax.experimental.pallas import tpu as pltpu
from jax.sharding import PartitionSpec as P

HD = 128
GROUP = 16
KL = 128
BLOCK = 128


def for_sending(x):

    def short(part):
        return part.astype(jnp.bfloat16) if part.dtype == jnp.float32 else part

    return jax.tree.map(short, x)


def passed_along(value, axis, steps):
    count = lax.axis_size(axis)
    pairs = [(source, (source + steps) % count) for source in range(count)]
    return lax.ppermute(value, axis, pairs)


def keep_state(current):
    return current


def ring_device(
    block_order, queries, keys, values, hyena_q, hyena_k, hyena_v, hyena_grad, filters, proj_weight
):
    seq_count = lax.axis_size("seq")
    my_index = lax.axis_index("seq")
    row_count = queries.shape[0]
    feature_width = queries.shape[1]
    head_count = feature_width // HD
    block_total = block_order.shape[0]
    offsets = jnp.arange(BLOCK, dtype=jnp.int32)
    block_ids = jnp.arange(block_total, dtype=jnp.int32)

    def block_positions(source):
        block_pair = lax.dynamic_slice_in_dim(block_order, 2 * source, 2)
        return jnp.concatenate([block_pair[0] * BLOCK + offsets, block_pair[1] * BLOCK + offsets])

    def holder_of(target):
        return jnp.sum(jnp.where(block_order == target, block_ids, 0))

    my_positions = block_positions(my_index)
    product_kv = (hyena_k.astype(jnp.float32) * hyena_v.astype(jnp.float32)).astype(jnp.bfloat16)
    product_dq = (hyena_grad.astype(jnp.float32) * hyena_q.astype(jnp.float32)).astype(jnp.bfloat16)
    my_blocks = [
        lax.dynamic_index_in_dim(block_order, 2 * my_index + portion, 0, keepdims=False)
        for portion in range(2)
    ]
    gathered_z, gathered_dc = (
        lax.all_gather(product_kv, "seq", axis=0, tiled=True),
        lax.all_gather(product_dq, "seq", axis=0, tiled=True),
    )
    group_count = filters.shape[0]
    channels = hyena_q.shape[1]
    out_rows = jnp.arange(BLOCK)[:, None, None]
    window_rows = jnp.arange(BLOCK + KL)[None, :, None]
    tap_ids = jnp.arange(KL)[None, None, :]
    causal_table = (out_rows + KL - window_rows == tap_ids).astype(jnp.float32)
    anti_table = (window_rows - out_rows == tap_ids).astype(jnp.float32)
    causal_toeplitz = jnp.einsum(
        "gj,tsj->gts", filters, causal_table, precision=lax.Precision.HIGHEST
    )
    anti_toeplitz = jnp.einsum("gj,tsj->gts", filters, anti_table, precision=lax.Precision.HIGHEST)

    def apply_groups(toeplitz, window):
        grouped = window.astype(jnp.float32).reshape(BLOCK + KL, group_count, GROUP)
        result = jnp.einsum("gts,sgk->tgk", toeplitz, grouped, precision=lax.Precision.HIGHEST)
        return result.reshape(BLOCK, channels)

    conv_parts = []
    back_parts = []
    for portion in range(2):
        block_id = my_blocks[portion]
        before = lax.dynamic_slice_in_dim(
            gathered_z, holder_of(block_id - 1) * BLOCK + BLOCK - KL, KL, 0
        )
        before = jnp.where(block_id >= 1, before, jnp.zeros_like(before))
        after = lax.dynamic_slice_in_dim(gathered_dc, holder_of(block_id + 1) * BLOCK, KL, 0)
        after = jnp.where(block_id + 1 < block_total, after, jnp.zeros_like(after))
        own_z = product_kv[portion * BLOCK : (portion + 1) * BLOCK]
        own_dc = product_dq[portion * BLOCK : (portion + 1) * BLOCK]
        conv_parts.append(apply_groups(causal_toeplitz, jnp.concatenate([before, own_z])))
        back_parts.append(apply_groups(anti_toeplitz, jnp.concatenate([own_dc, after])))
    convolved = jnp.concatenate(conv_parts)
    back_conv = jnp.concatenate(back_parts)
    stacked = jnp.stack(
        [
            hyena_grad.astype(jnp.float32) * convolved,
            back_conv * hyena_v.astype(jnp.float32),
            back_conv * hyena_k.astype(jnp.float32),
        ]
    ).astype(jnp.bfloat16)
    summed = lax.psum_scatter(
        jnp.einsum("mic,mtc->it", proj_weight, stacked, preferred_element_type=jnp.float32),
        "head",
        scatter_dimension=0,
        tiled=True,
    )
    input_grad = summed.T.astype(jnp.bfloat16)
    score_scale = HD ** (-0.5)
    query_heads = queries.reshape(row_count, head_count, HD)
    key_heads = keys.reshape(row_count, head_count, HD)
    value_heads = values.reshape(row_count, head_count, HD)
    grad_heads = input_grad.reshape(row_count, head_count, HD)

    def tile_scores(query_block, key_block, query_pos, key_pos):
        scores = (
            jnp.einsum("qhd,khd->hqk", query_block, key_block, preferred_element_type=jnp.float32)
            * score_scale
        )
        allowed = (key_pos[None, :] <= query_pos[:, None])[None]
        return (scores, allowed)

    def stat_update(running, key_block, value_block, source):
        key_pos = block_positions(source)
        active = jnp.min(key_pos) <= jnp.max(my_positions)

        def stat_accumulate(current):
            row_max, row_sum, row_dot = current
            scores, allowed = tile_scores(query_heads, key_block, my_positions, key_pos)
            masked = jnp.where(allowed, scores, -1e30)
            new_max = jnp.maximum(row_max, jnp.max(masked, axis=2))
            terms = jnp.where(allowed, jnp.exp(masked - new_max[:, :, None]), 0.0)
            prob_grad = jnp.einsum(
                "qhd,khd->hqk", grad_heads, value_block, preferred_element_type=jnp.float32
            )
            factor = jnp.exp(row_max - new_max)
            return (
                new_max,
                row_sum * factor + jnp.sum(terms, axis=2),
                row_dot * factor + jnp.sum(terms * prob_grad, axis=2),
            )

        return lax.cond(active, stat_accumulate, keep_state, running)

    initial = (
        jnp.full((head_count, row_count), -1e30, jnp.float32),
        jnp.zeros((head_count, row_count), jnp.float32),
        jnp.zeros((head_count, row_count), jnp.float32),
    )

    def tile_grads(
        query_block, grad_block, norm_block, delta_block, query_pos, key_block, value_block, key_pos
    ):
        scores, allowed = tile_scores(query_block, key_block, query_pos, key_pos)
        probabilities = jnp.where(allowed, jnp.exp(scores - norm_block[:, :, None]), 0.0)
        prob_grad = jnp.einsum(
            "qhd,khd->hqk", grad_block, value_block, preferred_element_type=jnp.float32
        )
        score_grad = probabilities * (prob_grad - delta_block[:, :, None])
        probs_low = probabilities.astype(jnp.bfloat16)
        score_low = score_grad.astype(jnp.bfloat16)
        add_query = (
            jnp.einsum("hqk,khd->qhd", score_low, key_block, preferred_element_type=jnp.float32)
            * score_scale
        )
        add_key = (
            jnp.einsum("hqk,qhd->khd", score_low, query_block, preferred_element_type=jnp.float32)
            * score_scale
        )
        add_value = jnp.einsum(
            "hqk,qhd->khd", probs_low, grad_block, preferred_element_type=jnp.float32
        )
        return (add_query, add_key, add_value)

    zero_rows = jnp.zeros((row_count, head_count, HD), jnp.float32)

    def move_stat_queries(pair):
        return jax.tree.map(
            lambda part, own: part.astype(own.dtype),
            passed_along(for_sending(pair), "seq", 1),
            pair,
        )

    def stat_turn(turn_index, loop_state):
        running, key_block, value_block = loop_state
        source = (my_index - turn_index) % seq_count
        running = stat_update(running, key_block, value_block, source)
        key_block, value_block = move_stat_queries((key_block, value_block))
        return (running, key_block, value_block)

    loop_state = lax.fori_loop(0, seq_count - 1, stat_turn, (initial, key_heads, value_heads))
    running = stat_update(
        loop_state[0], loop_state[1], loop_state[2], (my_index - (seq_count - 1)) % seq_count
    )
    log_norm = running[0] + jnp.log(running[1])
    row_delta = running[2] / running[1]

    def query_turn(turn_index, loop_state):
        query_block, grad_block, norm_block, delta_block, query_acc, key_acc, value_acc = loop_state
        source = (my_index - turn_index) % seq_count
        query_pos = block_positions(source)
        active = jnp.min(my_positions) <= jnp.max(query_pos)

        def query_accumulate(current):
            add_query, add_key, add_value = tile_grads(
                query_block,
                grad_block,
                norm_block,
                delta_block,
                query_pos,
                key_heads,
                value_heads,
                my_positions,
            )
            return (current[0] + add_query, current[1] + add_key, current[2] + add_value)

        query_acc, key_acc, value_acc = lax.cond(
            active, query_accumulate, keep_state, (query_acc, key_acc, value_acc)
        )
        query_block, grad_block = passed_along((query_block, grad_block), "seq", 1)
        norm_block, delta_block, query_acc = passed_along(
            (norm_block, delta_block, query_acc), "seq", 1
        )
        return (query_block, grad_block, norm_block, delta_block, query_acc, key_acc, value_acc)

    final_state = lax.fori_loop(
        0,
        seq_count,
        query_turn,
        (query_heads, grad_heads, log_norm, row_delta, zero_rows, zero_rows, zero_rows),
    )
    query_total = final_state[4]
    key_total = final_state[5]
    value_total = final_state[6]
    query_grad = query_total.reshape(row_count, feature_width).astype(jnp.bfloat16)
    key_grad = key_total.reshape(row_count, feature_width).astype(jnp.bfloat16)
    value_grad = value_total.reshape(row_count, feature_width).astype(jnp.bfloat16)
    return (input_grad, query_grad, key_grad, value_grad)


MESH = pl.DeviceIdType.MESH
VMEM_SPEC = pl.BlockSpec(memory_space=pltpu.VMEM)
SMEM_SPEC = pl.BlockSpec(memory_space=pltpu.SMEM)


def aligned(index, size):
    return pl.ds(pl.multiple_of(index * size, size), size)


def greet(me, n, head_peers=()):
    barrier = pltpu.get_barrier_semaphore()
    for step in range(1, n):
        pl.semaphore_signal(
            barrier, inc=1, device_id={"seq": lax.rem(me + step, n)}, device_id_type=MESH
        )
    for peer in head_peers:
        pl.semaphore_signal(barrier, inc=1, device_id={"head": peer}, device_id_type=MESH)
    pl.semaphore_wait(barrier, n - 1 + len(head_peers))


def exchange(n, me, rows, send_sem, recv_sem, own_sem):
    def parts(to_columns, src, dst, peer):
        if to_columns:
            return src.at[:, aligned(peer, HD)], dst.at[aligned(me, rows), :]
        return src.at[aligned(peer, rows), :], dst.at[:, aligned(me, HD)]

    def remote(tensor, to_columns, src, dst, step):
        peer = lax.rem(me + step, n)
        part, place = parts(to_columns, src, dst, peer)
        return pltpu.make_async_remote_copy(
            src_ref=part,
            dst_ref=place,
            send_sem=send_sem.at[tensor, step],
            recv_sem=recv_sem.at[tensor, step],
            device_id={"seq": peer},
            device_id_type=MESH,
        )

    def own(tensor, to_columns, src, dst):
        part, place = parts(to_columns, src, dst, me)
        return pltpu.make_async_copy(part, place, own_sem.at[tensor])

    def start(tensor, to_columns, src, dst):
        for step in range(1, n):
            remote(tensor, to_columns, src, dst, step).start()
        own(tensor, to_columns, src, dst).start()

    def wait(tensor, to_columns, src, dst):
        for step in range(1, n):
            remote(tensor, to_columns, src, dst, step).wait()
        own(tensor, to_columns, src, dst).wait()

    return remote, own, start, wait


def exchange_sems(tensors, n):
    return [
        pltpu.SemaphoreType.DMA((tensors, n)),
        pltpu.SemaphoreType.DMA((tensors, n)),
        pltpu.SemaphoreType.DMA((tensors,)),
    ]


def move_kernel(n, to_columns, count, *refs):
    sources, targets = refs[:count], refs[count : 2 * count]
    me = lax.axis_index("seq")
    rows = sources[0].shape[0] if to_columns else targets[0].shape[0]
    _, _, start, wait = exchange(n, me, rows, *refs[2 * count :])
    greet(me, n)
    for t in range(count):
        start(t, to_columns, sources[t], targets[t])
    for t in range(count):
        wait(t, to_columns, sources[t], targets[t])


def move(n, to_columns, arrays, collective_id):
    rows, columns = arrays[0].shape
    shape = (rows * n, columns // n) if to_columns else (rows // n, columns * n)
    count = len(arrays)
    return pl.pallas_call(
        functools.partial(move_kernel, n, to_columns, count),
        out_shape=[jax.ShapeDtypeStruct(shape, a.dtype) for a in arrays],
        in_specs=[VMEM_SPEC] * count,
        out_specs=[VMEM_SPEC] * count,
        scratch_shapes=exchange_sems(count, n),
        compiler_params=pltpu.CompilerParams(
            collective_id=collective_id, has_side_effects=True
        ),
    )(*arrays)


def hyena_kernel(
    n, heads, groups,
    before_ref, after_ref, hq_ref, hk_ref, hv_ref, hg_ref, causal_ref, anti_ref,
    q_ref, k_ref, v_ref, weight_ref,
    grad_ref, qc_ref, kc_ref, vc_ref, gc_ref,
    z_ref, dc_ref, conv_ref, dz_ref, zc, dcc, convc, dzc,
    causal_high, causal_low, anti_high, anti_low,
    stacked, weights, kept, pair_out, pair_in, line_out, line_in,
    send_sem, recv_sem, own_sem, weight_sem, pair_sem, line_sem,
):
    me = lax.axis_index("seq")
    head = lax.axis_index("head")
    rows, columns = z_ref.shape
    blocks = zc.shape[0] // BLOCK
    chips = heads // 2
    chip, core = head // 2, lax.rem(head, 2)
    partner = chip * 2 + 1 - core
    along = [lax.rem(chip + step, chips) for step in range(chips)]
    order = list(range(1, chips)) + [0]
    remote, own, start, wait = exchange(n, me, rows, send_sem, recv_sem, own_sem)

    def weight_copy(slot, goal, m):
        return pltpu.make_async_copy(
            weight_ref.at[m, aligned(goal, columns), :], weights.at[slot, m],
            weight_sem.at[slot, m],
        )

    for step in order:
        for mine in range(2):
            goal = along[step] * 2 + (core if mine else 1 - core)
            for m in range(3):
                weight_copy(2 * step + mine, goal, m).start()
    wide_of = lambda ref: ref[...].astype(jnp.float32)
    z_ref[...] = (wide_of(hk_ref) * wide_of(hv_ref)).astype(jnp.bfloat16)
    dc_ref[...] = (wide_of(hg_ref) * wide_of(hq_ref)).astype(jnp.bfloat16)
    greet(me, n, [partner] + [along[step] * 2 + core for step in range(1, chips)])
    start(0, True, z_ref, zc)
    start(1, True, dc_ref, dcc)

    window = 2 * BLOCK
    for base_ref, high, low in (
        (causal_ref, causal_high, causal_low), (anti_ref, anti_high, anti_low)
    ):
        for g in range(groups):
            base = jnp.broadcast_to(base_ref[g : g + 1, :], (BLOCK, window))
            table = pltpu.roll(base, 0, 1, stride=1, stride_axis=0)
            top = table.astype(jnp.bfloat16)
            high[:, g * window : (g + 1) * window] = top
            low[:, g * window : (g + 1) * window] = (table - top.astype(jnp.float32)).astype(
                jnp.bfloat16
            )

    lane_group = lax.broadcasted_iota(jnp.int32, (window, 2 * HD), 1) % HD // GROUP

    def filtered(source, neighbours, high, low, target, place, own_first):
        halves = []
        for half in range(2):
            block = place * 2 + half
            own_rows = source[aligned(block, BLOCK), :]
            picks = neighbours[aligned(block, blocks), :]
            other = source[:BLOCK, :] * picks[0:1, :]
            for b in range(1, blocks):
                other = other + source[b * BLOCK : (b + 1) * BLOCK, :] * picks[b : b + 1, :]
            pair = [own_rows, other] if own_first else [other, own_rows]
            halves.append(jnp.concatenate(pair, axis=0))
        wide = jnp.concatenate(halves, axis=1)
        stack = jnp.concatenate(
            [jnp.where(lane_group == g, wide, jnp.zeros_like(wide)) for g in range(groups)], axis=0
        )
        result = jnp.dot(high[...], stack, preferred_element_type=jnp.float32)
        result = result + jnp.dot(low[...], stack, preferred_element_type=jnp.float32)
        result = result.astype(target.dtype)
        target[aligned(place, rows), :] = jnp.concatenate(
            [result[:, :HD], result[:, HD:]], axis=0
        )

    def send_back(tensor, source, neighbours, high, low, target, out, own_first):
        def one(step, carry):
            filtered(source, neighbours, high, low, target, lax.rem(me + step, n), own_first)
            remote(tensor, False, target, out, step).start()
            return carry

        lax.fori_loop(1, n, one, 0)
        filtered(source, neighbours, high, low, target, me, own_first)
        own(tensor, False, target, out).start()

    wait(0, True, z_ref, zc)
    send_back(2, zc, before_ref, causal_high, causal_low, convc, conv_ref, False)
    wait(1, True, dc_ref, dcc)
    send_back(3, dcc, after_ref, anti_high, anti_low, dzc, dz_ref, True)
    attention = ((4, q_ref, qc_ref), (5, k_ref, kc_ref), (6, v_ref, vc_ref))
    for t, src, dst in attention:
        start(t, True, src, dst)
    wait(2, False, convc, conv_ref)
    stacked[0] = (wide_of(hg_ref) * wide_of(conv_ref)).astype(jnp.bfloat16)
    wait(3, False, dzc, dz_ref)
    stacked[1] = (wide_of(dz_ref) * wide_of(hv_ref)).astype(jnp.bfloat16)
    stacked[2] = (wide_of(dz_ref) * wide_of(hk_ref)).astype(jnp.bfloat16)

    def project(slot, goal, target):
        for m in range(3):
            weight_copy(slot, goal, m).wait()
        tile = 2 * BLOCK

        def one(j, carry):
            total = None
            for m in range(3):
                part = lax.dot_general(
                    stacked[m], weights[slot, m, aligned(j, tile), :],
                    (((1,), (1,)), ((), ())), preferred_element_type=jnp.float32,
                )
                total = part if total is None else total + part
            target[:, aligned(j, tile)] = total
            return carry

        lax.fori_loop(0, columns // tile, one, 0)

    def pair_copy(step):
        return pltpu.make_async_remote_copy(
            src_ref=pair_out.at[step], dst_ref=pair_in.at[step],
            send_sem=pair_sem.at[0, step], recv_sem=pair_sem.at[1, step],
            device_id={"head": partner}, device_id_type=MESH,
        )

    def line_copy(step):
        return pltpu.make_async_remote_copy(
            src_ref=line_out.at[step - 1], dst_ref=line_in.at[step - 1],
            send_sem=line_sem.at[0, step], recv_sem=line_sem.at[1, step],
            device_id={"head": along[step] * 2 + core}, device_id_type=MESH,
        )

    for step in order:
        project(2 * step, along[step] * 2 + 1 - core, pair_out.at[step])
        pair_copy(step).start()
        project(2 * step + 1, along[step] * 2 + core, kept)
        pair_copy(step).wait()
        if step:
            line_out[step - 1] = kept[...] + pair_in[step]
            line_copy(step).start()
    total = kept[...] + pair_in[0]
    for step in range(1, chips):
        line_copy(step).wait()
        total = total + line_in[step - 1]
    grad_ref[...] = total.astype(grad_ref.dtype)
    start(7, True, grad_ref, gc_ref)
    for t, src, dst in attention:
        wait(t, True, src, dst)
    wait(7, True, grad_ref, gc_ref)


def hyena(
    n, heads, before, after, hyena_q, hyena_k, hyena_v, hyena_grad, causal_base, anti_base,
    queries, keys, values, proj_weight,
):
    rows, columns = queries.shape
    groups = causal_base.shape[0]
    chips = heads // 2
    like = jax.ShapeDtypeStruct(queries.shape, jnp.bfloat16)
    moved = jax.ShapeDtypeStruct((rows * n, HD), jnp.bfloat16)
    table = pltpu.VMEM((BLOCK, groups * 2 * BLOCK), jnp.bfloat16)
    low = pltpu.VMEM((rows, columns), jnp.bfloat16)
    partial = lambda count: pltpu.VMEM((count, rows, columns), jnp.float32)
    return pl.pallas_call(
        functools.partial(hyena_kernel, n, heads, groups),
        out_shape=[like] + [moved] * 4,
        in_specs=[VMEM_SPEC] * 11 + [pl.BlockSpec(memory_space=pl.ANY)],
        out_specs=[VMEM_SPEC] * 5,
        scratch_shapes=[low] * 4
        + [pltpu.VMEM((rows * n, HD), jnp.bfloat16)] * 4
        + [table] * 4
        + [
            pltpu.VMEM((3, rows, columns), jnp.bfloat16),
            pltpu.VMEM((heads, 3, columns, columns), jnp.bfloat16),
            pltpu.VMEM((rows, columns), jnp.float32),
            partial(chips), partial(chips), partial(chips - 1), partial(chips - 1),
        ]
        + exchange_sems(8, n)
        + [
            pltpu.SemaphoreType.DMA((heads, 3)),
            pltpu.SemaphoreType.DMA((2, chips)),
            pltpu.SemaphoreType.DMA((2, chips)),
        ],
        compiler_params=pltpu.CompilerParams(
            collective_id=0, has_side_effects=True, vmem_limit_bytes=60 * 2**20
        ),
    )(
        before, after, hyena_q, hyena_k, hyena_v, hyena_grad, causal_base, anti_base,
        queries, keys, values, proj_weight,
    )


def attention_kernel(
    order_ref, holder_ref, q_ref, k_ref, v_ref, g_ref, dq_ref, dk_ref, dv_ref,
    ks, vs, kst, dq_sum, dk_sum, dv_sum,
):
    blocks = order_ref.shape[0]
    scale = HD ** (-0.5)
    tile = 2 * BLOCK
    for b in range(blocks):
        at = aligned(holder_ref[b], BLOCK)
        here = slice(b * BLOCK, (b + 1) * BLOCK)
        rows = k_ref[at, :]
        ks[here, :] = rows
        kst[:, here] = rows.T
        vs[here, :] = v_ref[at, :]
    contract_last = (((1,), (1,)), ((), ()))
    for i in reversed(range(blocks // 2)):
        width = (i + 1) * tile
        first = aligned(holder_ref[2 * i], BLOCK)
        second = aligned(holder_ref[2 * i + 1], BLOCK)
        q = jnp.concatenate([q_ref[first, :], q_ref[second, :]], axis=0)
        g = jnp.concatenate([g_ref[first, :], g_ref[second, :]], axis=0)
        scores = lax.dot_general(
            ks[:width, :], q, contract_last, preferred_element_type=jnp.float32
        ) * scale
        key_at = lax.broadcasted_iota(jnp.int32, (tile, tile), 0)
        query_at = lax.broadcasted_iota(jnp.int32, (tile, tile), 1)
        last = jnp.where(key_at <= query_at, scores[width - tile :], -1e30)
        if i:
            scores = jnp.concatenate([scores[: width - tile], last], axis=0)
        else:
            scores = last
        top = jnp.max(scores, axis=0, keepdims=True)
        terms = jnp.exp(scores - top)
        inverse = 1.0 / jnp.sum(terms, axis=0, keepdims=True)
        prob = terms * inverse
        prob_grad = lax.dot_general(
            vs[:width, :], g, contract_last, preferred_element_type=jnp.float32
        )
        delta = jnp.sum(prob * prob_grad, axis=0, keepdims=True)
        score_grad = (prob * (prob_grad - delta)).astype(jnp.bfloat16)
        add_value = jnp.dot(prob.astype(jnp.bfloat16), g, preferred_element_type=jnp.float32)
        add_key = jnp.dot(score_grad, q, preferred_element_type=jnp.float32)
        if i == blocks // 2 - 1:
            dv_sum[:width, :] = add_value
            dk_sum[:width, :] = add_key
        else:
            dv_sum[:width, :] += add_value
            dk_sum[:width, :] += add_key
        query_t = jnp.dot(kst[:, :width], score_grad, preferred_element_type=jnp.float32)
        dq_sum[i * tile : (i + 1) * tile, :] = query_t.T * scale
    for s in range(blocks):
        at = aligned(order_ref[s], BLOCK)
        here = slice(s * BLOCK, (s + 1) * BLOCK)
        dq_ref[here, :] = dq_sum[at, :].astype(dq_ref.dtype)
        dk_ref[here, :] = (dk_sum[at, :] * scale).astype(dk_ref.dtype)
        dv_ref[here, :] = dv_sum[at, :].astype(dv_ref.dtype)


def attention(order, holder, q, k, v, g):
    shape = jax.ShapeDtypeStruct(q.shape, jnp.bfloat16)
    low = pltpu.VMEM(q.shape, jnp.bfloat16)
    full = pltpu.VMEM(q.shape, jnp.float32)
    return pl.pallas_call(
        attention_kernel,
        out_shape=[shape] * 3,
        in_specs=[SMEM_SPEC] * 2 + [VMEM_SPEC] * 4,
        out_specs=[VMEM_SPEC] * 3,
        scratch_shapes=[low, low, pltpu.VMEM(q.shape[::-1], jnp.bfloat16), full, full, full],
    )(order, holder, q, k, v, g)


def column_device(
    block_order, queries, keys, values, hyena_q, hyena_k, hyena_v, hyena_grad, filters, proj_weight
):
    n = lax.axis_size("seq")
    me = lax.axis_index("seq")
    blocks = block_order.shape[0]
    ids = jnp.arange(blocks, dtype=jnp.int32)
    holder = jnp.sum(
        jnp.where(block_order[None, :] == ids[:, None], ids[None, :], 0), axis=1
    ).astype(jnp.int32)

    def neighbour(offset):
        found = (block_order[None, :] == block_order[:, None] + offset).astype(jnp.bfloat16)
        return jnp.broadcast_to(found.reshape(blocks * blocks, 1), (blocks * blocks, HD))

    groups = filters.shape[0] // n
    taps = lax.dynamic_slice_in_dim(filters, me * groups, groups, 0)
    anti_base = jnp.pad(taps, ((0, 0), (0, KL)))
    causal_base = jnp.pad(taps[:, ::-1], ((0, 0), (1, KL - 1)))
    heads = lax.axis_size("head")
    input_grad, qc, kc, vc, gc = hyena(
        n, heads, neighbour(-1), neighbour(1), hyena_q, hyena_k, hyena_v, hyena_grad,
        causal_base, anti_base, queries, keys, values, proj_weight,
    )
    grads = attention(block_order, holder, qc, kc, vc, gc)
    query_grad, key_grad, value_grad = move(n, False, list(grads), 2)
    return (input_grad, query_grad, key_grad, value_grad)


def per_device(*arrays):
    queries, filters = arrays[1], arrays[8]
    n = lax.axis_size("seq")
    whole_heads = queries.shape[1] == n * HD and queries.shape[0] == 2 * BLOCK
    paired = lax.axis_size("head") % 2 == 0 and lax.axis_size("head") > 2
    if whole_heads and paired and filters.shape[0] % n == 0 and KL == BLOCK == HD:
        return column_device(*arrays)
    return ring_device(*arrays)


def solution(mesh):
    placed = (
        P(),
        P("seq", "head"),
        P("seq", "head"),
        P("seq", "head"),
        P("seq", "head"),
        P("seq", "head"),
        P("seq", "head"),
        P("seq", "head"),
        P("head", None),
        P(None, None, "head"),
    )
    return jax.shard_map(
        per_device,
        mesh=mesh,
        in_specs=placed,
        out_specs=(P("seq", "head"), P("seq", "head"), P("seq", "head"), P("seq", "head")),
        check_vma=False,
    )
```

```python
import functools

import jax
import jax.numpy as jnp
from jax import lax
from jax.experimental import pallas as pl
from jax.experimental.pallas import tpu as pltpu
from jax.sharding import PartitionSpec as P

HD = 128
GROUP = 16
KL = 128
BLOCK = 128


def for_sending(x):

    def short(part):
        return part.astype(jnp.bfloat16) if part.dtype == jnp.float32 else part

    return jax.tree.map(short, x)


def passed_along(value, axis, steps):
    count = lax.axis_size(axis)
    pairs = [(source, (source + steps) % count) for source in range(count)]
    return lax.ppermute(value, axis, pairs)


def keep_state(current):
    return current


def ring_device(
    block_order, queries, keys, values, hyena_q, hyena_k, hyena_v, hyena_grad, filters, proj_weight
):
    seq_count = lax.axis_size("seq")
    my_index = lax.axis_index("seq")
    row_count = queries.shape[0]
    feature_width = queries.shape[1]
    head_count = feature_width // HD
    block_total = block_order.shape[0]
    offsets = jnp.arange(BLOCK, dtype=jnp.int32)
    block_ids = jnp.arange(block_total, dtype=jnp.int32)

    def block_positions(source):
        block_pair = lax.dynamic_slice_in_dim(block_order, 2 * source, 2)
        return jnp.concatenate([block_pair[0] * BLOCK + offsets, block_pair[1] * BLOCK + offsets])

    def holder_of(target):
        return jnp.sum(jnp.where(block_order == target, block_ids, 0))

    my_positions = block_positions(my_index)
    product_kv = (hyena_k.astype(jnp.float32) * hyena_v.astype(jnp.float32)).astype(jnp.bfloat16)
    product_dq = (hyena_grad.astype(jnp.float32) * hyena_q.astype(jnp.float32)).astype(jnp.bfloat16)
    my_blocks = [
        lax.dynamic_index_in_dim(block_order, 2 * my_index + portion, 0, keepdims=False)
        for portion in range(2)
    ]
    gathered_z, gathered_dc = (
        lax.all_gather(product_kv, "seq", axis=0, tiled=True),
        lax.all_gather(product_dq, "seq", axis=0, tiled=True),
    )
    group_count = filters.shape[0]
    channels = hyena_q.shape[1]
    out_rows = jnp.arange(BLOCK)[:, None, None]
    window_rows = jnp.arange(BLOCK + KL)[None, :, None]
    tap_ids = jnp.arange(KL)[None, None, :]
    causal_table = (out_rows + KL - window_rows == tap_ids).astype(jnp.float32)
    anti_table = (window_rows - out_rows == tap_ids).astype(jnp.float32)
    causal_toeplitz = jnp.einsum(
        "gj,tsj->gts", filters, causal_table, precision=lax.Precision.HIGHEST
    )
    anti_toeplitz = jnp.einsum("gj,tsj->gts", filters, anti_table, precision=lax.Precision.HIGHEST)

    def apply_groups(toeplitz, window):
        grouped = window.astype(jnp.float32).reshape(BLOCK + KL, group_count, GROUP)
        result = jnp.einsum("gts,sgk->tgk", toeplitz, grouped, precision=lax.Precision.HIGHEST)
        return result.reshape(BLOCK, channels)

    conv_parts = []
    back_parts = []
    for portion in range(2):
        block_id = my_blocks[portion]
        before = lax.dynamic_slice_in_dim(
            gathered_z, holder_of(block_id - 1) * BLOCK + BLOCK - KL, KL, 0
        )
        before = jnp.where(block_id >= 1, before, jnp.zeros_like(before))
        after = lax.dynamic_slice_in_dim(gathered_dc, holder_of(block_id + 1) * BLOCK, KL, 0)
        after = jnp.where(block_id + 1 < block_total, after, jnp.zeros_like(after))
        own_z = product_kv[portion * BLOCK : (portion + 1) * BLOCK]
        own_dc = product_dq[portion * BLOCK : (portion + 1) * BLOCK]
        conv_parts.append(apply_groups(causal_toeplitz, jnp.concatenate([before, own_z])))
        back_parts.append(apply_groups(anti_toeplitz, jnp.concatenate([own_dc, after])))
    convolved = jnp.concatenate(conv_parts)
    back_conv = jnp.concatenate(back_parts)
    stacked = jnp.stack(
        [
            hyena_grad.astype(jnp.float32) * convolved,
            back_conv * hyena_v.astype(jnp.float32),
            back_conv * hyena_k.astype(jnp.float32),
        ]
    ).astype(jnp.bfloat16)
    summed = lax.psum_scatter(
        jnp.einsum("mic,mtc->it", proj_weight, stacked, preferred_element_type=jnp.float32),
        "head",
        scatter_dimension=0,
        tiled=True,
    )
    input_grad = summed.T.astype(jnp.bfloat16)
    score_scale = HD ** (-0.5)
    query_heads = queries.reshape(row_count, head_count, HD)
    key_heads = keys.reshape(row_count, head_count, HD)
    value_heads = values.reshape(row_count, head_count, HD)
    grad_heads = input_grad.reshape(row_count, head_count, HD)

    def tile_scores(query_block, key_block, query_pos, key_pos):
        scores = (
            jnp.einsum("qhd,khd->hqk", query_block, key_block, preferred_element_type=jnp.float32)
            * score_scale
        )
        allowed = (key_pos[None, :] <= query_pos[:, None])[None]
        return (scores, allowed)

    def stat_update(running, key_block, value_block, source):
        key_pos = block_positions(source)
        active = jnp.min(key_pos) <= jnp.max(my_positions)

        def stat_accumulate(current):
            row_max, row_sum, row_dot = current
            scores, allowed = tile_scores(query_heads, key_block, my_positions, key_pos)
            masked = jnp.where(allowed, scores, -1e30)
            new_max = jnp.maximum(row_max, jnp.max(masked, axis=2))
            terms = jnp.where(allowed, jnp.exp(masked - new_max[:, :, None]), 0.0)
            prob_grad = jnp.einsum(
                "qhd,khd->hqk", grad_heads, value_block, preferred_element_type=jnp.float32
            )
            factor = jnp.exp(row_max - new_max)
            return (
                new_max,
                row_sum * factor + jnp.sum(terms, axis=2),
                row_dot * factor + jnp.sum(terms * prob_grad, axis=2),
            )

        return lax.cond(active, stat_accumulate, keep_state, running)

    initial = (
        jnp.full((head_count, row_count), -1e30, jnp.float32),
        jnp.zeros((head_count, row_count), jnp.float32),
        jnp.zeros((head_count, row_count), jnp.float32),
    )

    def tile_grads(
        query_block, grad_block, norm_block, delta_block, query_pos, key_block, value_block, key_pos
    ):
        scores, allowed = tile_scores(query_block, key_block, query_pos, key_pos)
        probabilities = jnp.where(allowed, jnp.exp(scores - norm_block[:, :, None]), 0.0)
        prob_grad = jnp.einsum(
            "qhd,khd->hqk", grad_block, value_block, preferred_element_type=jnp.float32
        )
        score_grad = probabilities * (prob_grad - delta_block[:, :, None])
        probs_low = probabilities.astype(jnp.bfloat16)
        score_low = score_grad.astype(jnp.bfloat16)
        add_query = (
            jnp.einsum("hqk,khd->qhd", score_low, key_block, preferred_element_type=jnp.float32)
            * score_scale
        )
        add_key = (
            jnp.einsum("hqk,qhd->khd", score_low, query_block, preferred_element_type=jnp.float32)
            * score_scale
        )
        add_value = jnp.einsum(
            "hqk,qhd->khd", probs_low, grad_block, preferred_element_type=jnp.float32
        )
        return (add_query, add_key, add_value)

    zero_rows = jnp.zeros((row_count, head_count, HD), jnp.float32)

    def move_stat_queries(pair):
        return jax.tree.map(
            lambda part, own: part.astype(own.dtype),
            passed_along(for_sending(pair), "seq", 1),
            pair,
        )

    def stat_turn(turn_index, loop_state):
        running, key_block, value_block = loop_state
        source = (my_index - turn_index) % seq_count
        running = stat_update(running, key_block, value_block, source)
        key_block, value_block = move_stat_queries((key_block, value_block))
        return (running, key_block, value_block)

    loop_state = lax.fori_loop(0, seq_count - 1, stat_turn, (initial, key_heads, value_heads))
    running = stat_update(
        loop_state[0], loop_state[1], loop_state[2], (my_index - (seq_count - 1)) % seq_count
    )
    log_norm = running[0] + jnp.log(running[1])
    row_delta = running[2] / running[1]

    def query_turn(turn_index, loop_state):
        query_block, grad_block, norm_block, delta_block, query_acc, key_acc, value_acc = loop_state
        source = (my_index - turn_index) % seq_count
        query_pos = block_positions(source)
        active = jnp.min(my_positions) <= jnp.max(query_pos)

        def query_accumulate(current):
            add_query, add_key, add_value = tile_grads(
                query_block,
                grad_block,
                norm_block,
                delta_block,
                query_pos,
                key_heads,
                value_heads,
                my_positions,
            )
            return (current[0] + add_query, current[1] + add_key, current[2] + add_value)

        query_acc, key_acc, value_acc = lax.cond(
            active, query_accumulate, keep_state, (query_acc, key_acc, value_acc)
        )
        query_block, grad_block = passed_along((query_block, grad_block), "seq", 1)
        norm_block, delta_block, query_acc = passed_along(
            (norm_block, delta_block, query_acc), "seq", 1
        )
        return (query_block, grad_block, norm_block, delta_block, query_acc, key_acc, value_acc)

    final_state = lax.fori_loop(
        0,
        seq_count,
        query_turn,
        (query_heads, grad_heads, log_norm, row_delta, zero_rows, zero_rows, zero_rows),
    )
    query_total = final_state[4]
    key_total = final_state[5]
    value_total = final_state[6]
    query_grad = query_total.reshape(row_count, feature_width).astype(jnp.bfloat16)
    key_grad = key_total.reshape(row_count, feature_width).astype(jnp.bfloat16)
    value_grad = value_total.reshape(row_count, feature_width).astype(jnp.bfloat16)
    return (input_grad, query_grad, key_grad, value_grad)


MESH = pl.DeviceIdType.MESH
VMEM_SPEC = pl.BlockSpec(memory_space=pltpu.VMEM)
SMEM_SPEC = pl.BlockSpec(memory_space=pltpu.SMEM)


def aligned(index, size):
    return pl.ds(pl.multiple_of(index * size, size), size)


def signal_peers(me, n, head_peers=()):
    barrier = pltpu.get_barrier_semaphore()
    for step in range(1, n):
        pl.semaphore_signal(
            barrier, inc=1, device_id={"seq": lax.rem(me + step, n)}, device_id_type=MESH
        )
    for peer in head_peers:
        pl.semaphore_signal(barrier, inc=1, device_id={"head": peer}, device_id_type=MESH)


def greet(me, n, head_peers=()):
    signal_peers(me, n, head_peers)
    pl.semaphore_wait(pltpu.get_barrier_semaphore(), n - 1 + len(head_peers))


def exchange(n, me, rows, send_sem, recv_sem, own_sem):
    def parts(to_columns, src, dst, peer):
        if to_columns:
            return src.at[:, aligned(peer, HD)], dst.at[aligned(me, rows), :]
        return src.at[aligned(peer, rows), :], dst.at[:, aligned(me, HD)]

    def remote(tensor, to_columns, src, dst, step):
        peer = lax.rem(me + step, n)
        part, place = parts(to_columns, src, dst, peer)
        return pltpu.make_async_remote_copy(
            src_ref=part,
            dst_ref=place,
            send_sem=send_sem.at[tensor, step],
            recv_sem=recv_sem.at[tensor, step],
            device_id={"seq": peer},
            device_id_type=MESH,
        )

    def own(tensor, to_columns, src, dst):
        part, place = parts(to_columns, src, dst, me)
        return pltpu.make_async_copy(part, place, own_sem.at[tensor])

    def start(tensor, to_columns, src, dst):
        for step in range(1, n):
            remote(tensor, to_columns, src, dst, step).start()
        own(tensor, to_columns, src, dst).start()

    def wait(tensor, to_columns, src, dst):
        for step in range(1, n):
            remote(tensor, to_columns, src, dst, step).wait()
        own(tensor, to_columns, src, dst).wait()

    return remote, own, start, wait


def exchange_sems(tensors, n):
    return [
        pltpu.SemaphoreType.DMA((tensors, n)),
        pltpu.SemaphoreType.DMA((tensors, n)),
        pltpu.SemaphoreType.DMA((tensors,)),
    ]


def hyena_kernel(
    n, heads, groups,
    picks_ref, hq_ref, hk_ref, hv_ref, hg_ref, base_ref,
    q_ref, k_ref, v_ref, weight_ref,
    grad_ref, qc_ref, kc_ref, vc_ref, gc_ref,
    z_ref, dc_ref, conv_ref, dz_ref, zc, dcc, convc, dzc,
    causal_high, causal_low, anti_high, anti_low,
    stacked, weights, kept, pair_out, pair_in, line_out, line_in,
    send_sem, recv_sem, own_sem, weight_sem, pair_sem, line_sem,
):
    me = lax.axis_index("seq")
    head = lax.axis_index("head")
    rows, columns = z_ref.shape
    blocks = zc.shape[0] // BLOCK
    chips = heads // 2
    chip, core = head // 2, lax.rem(head, 2)
    partner = chip * 2 + 1 - core
    along = [lax.rem(chip + step, chips) for step in range(chips)]
    order = list(range(1, chips)) + [0]
    remote, own, start, wait = exchange(n, me, rows, send_sem, recv_sem, own_sem)

    def weight_copy(slot, goal, m):
        return pltpu.make_async_copy(
            weight_ref.at[m, aligned(goal, columns), :], weights.at[slot, m],
            weight_sem.at[slot, m],
        )

    for step in order:
        for mine in range(2):
            goal = along[step] * 2 + (core if mine else 1 - core)
            for m in range(3):
                weight_copy(2 * step + mine, goal, m).start()
    wide_of = lambda ref: ref[...].astype(jnp.float32)
    z_ref[...] = (wide_of(hk_ref) * wide_of(hv_ref)).astype(jnp.bfloat16)
    dc_ref[...] = (wide_of(hg_ref) * wide_of(hq_ref)).astype(jnp.bfloat16)
    greet(me, n, [partner] + [along[step] * 2 + core for step in range(1, chips)])
    start(0, True, z_ref, zc)
    start(1, True, dc_ref, dcc)

    window = 2 * BLOCK
    before_ref = picks_ref.at[: blocks * blocks, :]
    after_ref = picks_ref.at[blocks * blocks :, :]
    for at, high, low in ((0, causal_high, causal_low), (groups, anti_high, anti_low)):
        for g in range(groups):
            base = jnp.broadcast_to(base_ref[at + g : at + g + 1, :], (BLOCK, window))
            table = pltpu.roll(base, 0, 1, stride=1, stride_axis=0)
            top = table.astype(jnp.bfloat16)
            high[:, g * window : (g + 1) * window] = top
            low[:, g * window : (g + 1) * window] = (table - top.astype(jnp.float32)).astype(
                jnp.bfloat16
            )

    lane_group = lax.broadcasted_iota(jnp.int32, (window, 2 * HD), 1) % HD // GROUP

    def filtered(source, neighbours, high, low, target, place, own_first):
        halves = []
        for half in range(2):
            block = place * 2 + half
            own_rows = source[aligned(block, BLOCK), :]
            picks = neighbours[aligned(block, blocks), :]
            other = source[:BLOCK, :] * picks[0:1, :]
            for b in range(1, blocks):
                other = other + source[b * BLOCK : (b + 1) * BLOCK, :] * picks[b : b + 1, :]
            pair = [own_rows, other] if own_first else [other, own_rows]
            halves.append(jnp.concatenate(pair, axis=0))
        wide = jnp.concatenate(halves, axis=1)
        stack = jnp.concatenate(
            [jnp.where(lane_group == g, wide, jnp.zeros_like(wide)) for g in range(groups)], axis=0
        )
        result = jnp.dot(high[...], stack, preferred_element_type=jnp.float32)
        result = result + jnp.dot(low[...], stack, preferred_element_type=jnp.float32)
        result = result.astype(target.dtype)
        target[aligned(place, rows), :] = jnp.concatenate(
            [result[:, :HD], result[:, HD:]], axis=0
        )

    def send_back(tensor, source, neighbours, high, low, target, out, own_first):
        def one(step, carry):
            filtered(source, neighbours, high, low, target, lax.rem(me + step, n), own_first)
            remote(tensor, False, target, out, step).start()
            return carry

        lax.fori_loop(1, n, one, 0)
        filtered(source, neighbours, high, low, target, me, own_first)
        own(tensor, False, target, out).start()

    wait(0, True, z_ref, zc)
    send_back(2, zc, before_ref, causal_high, causal_low, convc, conv_ref, False)
    wait(1, True, dc_ref, dcc)
    send_back(3, dcc, after_ref, anti_high, anti_low, dzc, dz_ref, True)
    attention = ((4, q_ref, qc_ref), (5, k_ref, kc_ref), (6, v_ref, vc_ref))
    for t, src, dst in attention:
        start(t, True, src, dst)
    wait(2, False, convc, conv_ref)
    stacked[0] = (wide_of(hg_ref) * wide_of(conv_ref)).astype(jnp.bfloat16)
    wait(3, False, dzc, dz_ref)
    stacked[1] = (wide_of(dz_ref) * wide_of(hv_ref)).astype(jnp.bfloat16)
    stacked[2] = (wide_of(dz_ref) * wide_of(hk_ref)).astype(jnp.bfloat16)

    def project(slot, goal, target):
        for m in range(3):
            weight_copy(slot, goal, m).wait()
        tile = 2 * BLOCK

        def one(j, carry):
            total = None
            for m in range(3):
                part = lax.dot_general(
                    stacked[m], weights[slot, m, aligned(j, tile), :],
                    (((1,), (1,)), ((), ())), preferred_element_type=jnp.float32,
                )
                total = part if total is None else total + part
            target[:, aligned(j, tile)] = total
            return carry

        lax.fori_loop(0, columns // tile, one, 0)

    def pair_copy(step):
        return pltpu.make_async_remote_copy(
            src_ref=pair_out.at[step], dst_ref=pair_in.at[step],
            send_sem=pair_sem.at[0, step], recv_sem=pair_sem.at[1, step],
            device_id={"head": partner}, device_id_type=MESH,
        )

    def line_copy(step):
        return pltpu.make_async_remote_copy(
            src_ref=line_out.at[step - 1], dst_ref=line_in.at[step - 1],
            send_sem=line_sem.at[0, step], recv_sem=line_sem.at[1, step],
            device_id={"head": along[step] * 2 + core}, device_id_type=MESH,
        )

    for step in order:
        project(2 * step, along[step] * 2 + 1 - core, pair_out.at[step])
        pair_copy(step).start()
        project(2 * step + 1, along[step] * 2 + core, kept)
        pair_copy(step).wait()
        if step:
            line_out[step - 1] = kept[...] + pair_in[step]
            line_copy(step).start()
    total = kept[...] + pair_in[0]
    for step in range(1, chips):
        line_copy(step).wait()
        total = total + line_in[step - 1]
    grad_ref[...] = total.astype(grad_ref.dtype)
    start(7, True, grad_ref, gc_ref)
    for t, src, dst in attention:
        wait(t, True, src, dst)
    wait(7, True, grad_ref, gc_ref)


def hyena(
    n, heads, picks, hyena_q, hyena_k, hyena_v, hyena_grad, bases,
    queries, keys, values, proj_weight,
):
    rows, columns = queries.shape
    groups = bases.shape[0] // 2
    chips = heads // 2
    like = jax.ShapeDtypeStruct(queries.shape, jnp.bfloat16)
    moved = jax.ShapeDtypeStruct((rows * n, HD), jnp.bfloat16)
    table = pltpu.VMEM((BLOCK, groups * 2 * BLOCK), jnp.bfloat16)
    low = pltpu.VMEM((rows, columns), jnp.bfloat16)
    partial = lambda count: pltpu.VMEM((count, rows, columns), jnp.float32)
    return pl.pallas_call(
        functools.partial(hyena_kernel, n, heads, groups),
        out_shape=[like] + [moved] * 4,
        in_specs=[VMEM_SPEC] * 9 + [pl.BlockSpec(memory_space=pl.ANY)],
        out_specs=[VMEM_SPEC] * 5,
        scratch_shapes=[low] * 4
        + [pltpu.VMEM((rows * n, HD), jnp.bfloat16)] * 4
        + [table] * 4
        + [
            pltpu.VMEM((3, rows, columns), jnp.bfloat16),
            pltpu.VMEM((heads, 3, columns, columns), jnp.bfloat16),
            pltpu.VMEM((rows, columns), jnp.float32),
            partial(chips), partial(chips), partial(chips - 1), partial(chips - 1),
        ]
        + exchange_sems(8, n)
        + [
            pltpu.SemaphoreType.DMA((heads, 3)),
            pltpu.SemaphoreType.DMA((2, chips)),
            pltpu.SemaphoreType.DMA((2, chips)),
        ],
        compiler_params=pltpu.CompilerParams(
            collective_id=0, has_side_effects=True, vmem_limit_bytes=60 * 2**20
        ),
    )(
        picks, hyena_q, hyena_k, hyena_v, hyena_grad, bases,
        queries, keys, values, proj_weight,
    )


def attention_kernel(
    n, order_ref, holder_ref, q_ref, k_ref, v_ref, g_ref, dq_ref, dk_ref, dv_ref,
    ks, vs, kst, prob, dq_sum, dk_sum, dv_sum, dq_low, dk_low, dv_low, send_sem, recv_sem, own_sem,
):
    me = lax.axis_index("seq")
    blocks = order_ref.shape[0]
    _, _, start, wait = exchange(n, me, dq_ref.shape[0], send_sem, recv_sem, own_sem)
    signal_peers(me, n)
    scale = HD ** (-0.5)
    tile = 2 * BLOCK
    contract_last = (((1,), (1,)), ((), ()))
    for b in range(blocks):
        here = slice(b * BLOCK, (b + 1) * BLOCK)
        rows = k_ref[holder_ref[b]]
        ks[here, :] = rows
        kst[:, here] = rows.T
        vs[here, :] = v_ref[holder_ref[b]]

    def pair(ref, i):
        return jnp.concatenate([ref[holder_ref[2 * i]], ref[holder_ref[2 * i + 1]]], axis=0)

    def add(total, value, i):
        value = value.reshape(2 * i + 2, BLOCK, HD)
        if i == blocks // 2 - 1:
            total[...] = value
        else:
            total[: 2 * i + 2] += value

    def stored(i):
        return slice(tile * i * (i + 1) // 2, tile * (i + 1) * (i + 2) // 2)

    def give(total, factor, low):
        for s in range(blocks):
            rows = total[order_ref[s]]
            rows = rows if factor is None else rows * factor
            low[s * BLOCK : (s + 1) * BLOCK, :] = rows.astype(low.dtype)

    for i in reversed(range(blocks // 2)):
        width = (i + 1) * tile
        q = pair(q_ref, i)
        scores = lax.dot_general(
            ks[:width, :], q, contract_last, preferred_element_type=jnp.float32
        ) * scale
        key_at = lax.broadcasted_iota(jnp.int32, (tile, tile), 0)
        query_at = lax.broadcasted_iota(jnp.int32, (tile, tile), 1)
        last = jnp.where(key_at <= query_at, scores[width - tile :], -1e30)
        scores = jnp.concatenate([scores[: width - tile], last], axis=0) if i else last
        terms = jnp.exp(scores - jnp.max(scores, axis=0, keepdims=True))
        chance = terms * (1.0 / jnp.sum(terms, axis=0, keepdims=True))
        prob[stored(i), :] = chance
        add(
            dv_sum,
            jnp.dot(chance.astype(jnp.bfloat16), pair(g_ref, i), preferred_element_type=jnp.float32),
            i,
        )
    give(dv_sum, None, dv_low)
    pl.semaphore_wait(pltpu.get_barrier_semaphore(), n - 1)
    start(0, False, dv_low, dv_ref)
    for i in reversed(range(blocks // 2)):
        width = (i + 1) * tile
        prob_grad = lax.dot_general(
            vs[:width, :], pair(g_ref, i), contract_last, preferred_element_type=jnp.float32
        )
        chance = prob[stored(i), :]
        delta = jnp.sum(chance * prob_grad, axis=0, keepdims=True)
        score_grad = (chance * (prob_grad - delta)).astype(jnp.bfloat16)
        add(
            dk_sum,
            jnp.dot(score_grad, pair(q_ref, i), preferred_element_type=jnp.float32),
            i,
        )
        query_t = jnp.dot(kst[:, :width], score_grad, preferred_element_type=jnp.float32)
        dq_sum[2 * i : 2 * i + 2] = (query_t.T * scale).reshape(2, BLOCK, HD)
    give(dq_sum, None, dq_low)
    start(1, False, dq_low, dq_ref)
    give(dk_sum, scale, dk_low)
    start(2, False, dk_low, dk_ref)
    wait(0, False, dv_low, dv_ref)
    wait(1, False, dq_low, dq_ref)
    wait(2, False, dk_low, dk_ref)


def attention(n, order, holder, *tensors):
    rows = tensors[0].shape[0]
    blocks = rows // BLOCK
    low = pltpu.VMEM((rows, HD), jnp.bfloat16)
    full = pltpu.VMEM((blocks, BLOCK, HD), jnp.float32)
    tiles = rows // (2 * BLOCK)
    stored = 2 * BLOCK * tiles * (tiles + 1) // 2
    return pl.pallas_call(
        functools.partial(attention_kernel, n),
        out_shape=[jax.ShapeDtypeStruct((rows // n, HD * n), jnp.bfloat16)] * 3,
        in_specs=[SMEM_SPEC] * 2 + [VMEM_SPEC] * 4,
        out_specs=[VMEM_SPEC] * 3,
        scratch_shapes=[low, low, pltpu.VMEM((HD, rows), jnp.bfloat16)]
        + [pltpu.VMEM((stored, 2 * BLOCK), jnp.float32)]
        + [full] * 3
        + [low] * 3
        + exchange_sems(3, n),
        compiler_params=pltpu.CompilerParams(
            collective_id=1, has_side_effects=True, vmem_limit_bytes=50 * 2**20
        ),
    )(order, holder, *[t.reshape(blocks, BLOCK, HD) for t in tensors])


def land_kernel(count, *refs):
    for source, target in zip(refs[:count], refs[count:]):
        target[...] = source[...]


def land(*arrays):
    count = len(arrays)
    return pl.pallas_call(
        functools.partial(land_kernel, count),
        out_shape=[jax.ShapeDtypeStruct(a.shape, a.dtype) for a in arrays],
        in_specs=[VMEM_SPEC] * count,
        out_specs=[VMEM_SPEC] * count,
    )(*arrays)


def column_device(
    block_order, queries, keys, values, hyena_q, hyena_k, hyena_v, hyena_grad, filters, proj_weight
):
    n = lax.axis_size("seq")
    me = lax.axis_index("seq")
    blocks = block_order.shape[0]
    ids = jnp.arange(blocks, dtype=jnp.int32)
    holder = jnp.sum(
        jnp.where(block_order[None, :] == ids[:, None], ids[None, :], 0), axis=1
    ).astype(jnp.int32)

    wanted = jnp.concatenate([block_order - 1, block_order + 1])
    found = wanted[:, None, None] == block_order[None, :, None]
    picks = jnp.broadcast_to(found, (2 * blocks, blocks, HD)).astype(jnp.bfloat16)
    picks = picks.reshape(2 * blocks * blocks, HD)
    groups = filters.shape[0] // n
    taps = lax.dynamic_slice_in_dim(filters, me * groups, groups, 0)
    gap = jnp.zeros((groups, 1), taps.dtype)
    bases = jnp.concatenate(
        [
            jnp.concatenate([gap, taps[:, ::-1], jnp.zeros((groups, KL - 1), taps.dtype)], axis=1),
            jnp.concatenate([taps, jnp.zeros_like(taps)], axis=1),
        ],
        axis=0,
    )
    heads = lax.axis_size("head")
    input_grad, qc, kc, vc, gc = hyena(
        n, heads, picks, hyena_q, hyena_k, hyena_v, hyena_grad, bases, queries, keys, values, proj_weight,
    )
    grads = attention(n, block_order, holder, qc, kc, vc, gc)
    return tuple(land(input_grad, *grads))


def per_device(*arrays):
    queries, filters = arrays[1], arrays[8]
    n = lax.axis_size("seq")
    whole_heads = queries.shape[1] == n * HD and queries.shape[0] == 2 * BLOCK
    paired = lax.axis_size("head") % 2 == 0 and lax.axis_size("head") > 2
    if whole_heads and paired and filters.shape[0] % n == 0 and KL == BLOCK == HD:
        return column_device(*arrays)
    return ring_device(*arrays)


def solution(mesh):
    placed = (
        P(),
        P("seq", "head"),
        P("seq", "head"),
        P("seq", "head"),
        P("seq", "head"),
        P("seq", "head"),
        P("seq", "head"),
        P("seq", "head"),
        P("head", None),
        P(None, None, "head"),
    )
    return jax.shard_map(
        per_device,
        mesh=mesh,
        in_specs=placed,
        out_specs=(P("seq", "head"), P("seq", "head"), P("seq", "head"), P("seq", "head")),
        check_vma=False,
    )
```
